32 devices in a mesh: grp: 2 (over x), refl: 16 (over z, y, core).
Axes of the slice: x: 2, y: 2, z: 4, core: 2. Of those that a mesh axis runs over, the one named last changes fastest.
Arguments:
- feed_plane: float32 [4, 2048], P('grp', 'refl'), parts along dimension 0, may hold values from -3 to 3
- feed_height: float32 [4096], P(('grp', 'refl')), parts along dimension 0, may hold values from 20 to 24
- feed_weights: bfloat16 [2048, 256], P('refl', 'grp'), parts along dimension 1, may hold values from -0.125 to 0.125
- point_plane: float32 [4, 4096], P('grp', 'refl'), parts along dimension 0, may hold values from -35 to 35
- point_height: float32 [8192], P(('grp', 'refl')), parts along dimension 0, may hold values from 0 to 4
- patch_factor: float32 [8192], P(('grp', 'refl')), parts along dimension 0, may hold values from 0.3 to 3
- direction_cosines: float32 [2, 2048], P(None, 'refl'), may hold values from -0.3 to 0.3
Outputs:
- pattern: float32 [2048, 256], P('refl', 'grp'), parts along dimension 1
The draws below stay inside these ranges and needn't reach their ends.
There are 2 independent parts, one for each index of `grp`. The reference program is written for one: setup_inputs(seed, part) draws one part's arguments, and reference() takes and returns one part's arrays. A program takes and returns all parts, laid end to end along the dimension named above; an argument that names none is the same for every part. Nothing has to cross between parts.
All inputs are finite; a program needn't handle non-finite values.
Results may differ from the reference program's by a relative error of at most 0.0047.
Values may be sent and summed in bfloat16 or wider, within the bound.
A program may use at most 64 MiB of HBM per device.

```python
import math
import jax
import jax.numpy as jnp
from jax import lax

B = 64
P_DEV = 256
R_DEV = 128
S = 2048
P_SIZE = 4096
R = 2048


def block_levels(own_key, shape, cuts, low, high):
    gain, own = 1.0, jax.random.fold_in(own_key, 6)
    for axis_at, shards_of in cuts:
        steps = jnp.exp(jax.random.uniform(jax.random.fold_in(own, axis_at), (shards_of,), jnp.float32, low / len(cuts), high / len(cuts)))
        gain = gain * jnp.repeat(steps, shape[axis_at] // shards_of).reshape([-1 if axis == axis_at else 1 for axis in range(len(shape))])
    return gain


def gaussian(stream_key, shape, scale, most, split=(), held_as=jnp.bfloat16):
    level = block_levels(stream_key, shape, split, -0.22, 0.18) if split else 1.0
    result = jax.random.normal(stream_key, shape, jnp.float32) * scale * level
    return jnp.minimum(jnp.maximum(result, -most), most).astype(held_as)


def setup_inputs(seed: int = 0, part: int = 0) -> dict:
    key_of = jax.random.split(jax.random.key(seed), 8)
    part_splits = jax.random.split(jax.random.fold_in(key_of[7], part), 8)
    return {
        "feed_plane": jnp.clip(jax.random.uniform(part_splits[0], (2, S), jnp.float32, -3.0, 3.0) * block_levels(part_splits[0], (2, S), ((1, 16),), -0.4, 0.0), -3.0, 3.0),
        "feed_height": jnp.clip(20.0 + 4.0 * jax.random.uniform(part_splits[1], (S,), jnp.float32) ** block_levels(part_splits[1], (S,), ((0, 16),), -0.2, 0.2), 20.0, 24.0),
        "feed_weights": gaussian(part_splits[2], (S, 2 * B), S ** -0.5, 0.125, ((0, 16),)),
        "point_plane": jnp.clip(jax.random.uniform(part_splits[3], (2, P_SIZE), jnp.float32, -35.0, 35.0) * block_levels(part_splits[3], (2, P_SIZE), ((1, 16),), -0.4, 0.0), -35.0, 35.0),
        "point_height": jnp.clip(4.0 * jax.random.uniform(part_splits[4], (P_SIZE,), jnp.float32) ** block_levels(part_splits[4], (P_SIZE,), ((0, 16),), -0.2, 0.2), 0.0, 4.0),
        "patch_factor": jnp.clip(jnp.exp(math.log(3.0) - 2.3025851 * jax.random.uniform(part_splits[5], (P_SIZE,), jnp.float32) ** block_levels(part_splits[5], (P_SIZE,), ((0, 16),), -0.2, 0.2)), 0.3, 3.0),
        "direction_cosines": jnp.clip(jax.random.uniform(key_of[6], (2, R), jnp.float32, -0.3, 0.3) * block_levels(key_of[6], (2, R), ((1, 16),), -0.4, 0.0), -0.3, 0.3),
    }


TWO_PI = 2.0 * math.pi
RANGE_REF = 20.0

def rotate(columns):
    half = columns.shape[1] // 2
    return jnp.concatenate([-columns[:, half:], columns[:, :half]], axis=1)

def green_tile(point_plane, point_height, feed_plane, feed_height):
    across = point_plane[0][:, None] - feed_plane[0][None, :]
    along = point_plane[1][:, None] - feed_plane[1][None, :]
    height = feed_height[None, :] - point_height[:, None]
    squared = across * across + along * along + height * height
    distance = jnp.sqrt(squared)
    amplitude = RANGE_REF * height / squared
    turning = TWO_PI * distance
    return ((amplitude * jnp.cos(turning)).astype(jnp.bfloat16), (-amplitude * jnp.sin(turning)).astype(jnp.bfloat16))

def incident_rows(point_plane, point_height, feed_plane, feed_height, weights, weights_turned):
    in_phase, quadrature = green_tile(point_plane, point_height, feed_plane, feed_height)
    return jnp.dot(in_phase, weights, preferred_element_type=jnp.float32) + jnp.dot(quadrature, weights_turned, preferred_element_type=jnp.float32)

def far_kernel(cosines, point_plane, point_height):
    normal = jnp.sqrt(1.0 - cosines[0] * cosines[0] - cosines[1] * cosines[1])
    turning = TWO_PI * (cosines[0][:, None] * point_plane[0][None, :] + cosines[1][:, None] * point_plane[1][None, :] + normal[:, None] * point_height[None, :])
    return (jnp.cos(turning).astype(jnp.bfloat16), jnp.sin(turning).astype(jnp.bfloat16))

def radiate_rows(cosines, point_plane, point_height, currents, currents_turned):
    in_phase, quadrature = far_kernel(cosines, point_plane, point_height)
    return jnp.dot(in_phase, currents, preferred_element_type=jnp.float32) + jnp.dot(quadrature, currents_turned, preferred_element_type=jnp.float32)

def reference(feed_plane, feed_height, feed_weights, point_plane, point_height, patch_factor, direction_cosines):
    weights_turned = rotate(feed_weights)
    point_count = point_plane.shape[1]
    blocks = point_count // P_DEV
    plane_blocks = point_plane.reshape(2, blocks, P_DEV).transpose(1, 0, 2)
    height_blocks = point_height.reshape(blocks, P_DEV)
    incident = lax.map(lambda pair: incident_rows(pair[0], pair[1], feed_plane, feed_height, feed_weights, weights_turned), (plane_blocks, height_blocks)).reshape(point_count, 2 * B)
    norm_scale = 1.0 / math.sqrt(point_count)
    currents = (incident * (patch_factor * norm_scale)[:, None]).astype(jnp.bfloat16)
    currents_turned = rotate(currents)
    direction_count = direction_cosines.shape[1]
    dir_blocks = direction_count // R_DEV
    cosine_blocks = direction_cosines.reshape(2, dir_blocks, R_DEV).transpose(1, 0, 2)
    pattern = lax.map(lambda cosines: radiate_rows(cosines, point_plane, point_height, currents, currents_turned), cosine_blocks)
    return pattern.reshape(direction_count, 2 * B)
```

```python
import functools
import math

import jax
import jax.numpy as jnp
from jax import lax
from jax.experimental import pallas as pl
from jax.experimental.pallas import tpu as pltpu
from jax.sharding import PartitionSpec as P

RANGE_REF = 20.0
GROUP = 4
LANES = 128
ROWS = 32
MESH = pl.DeviceIdType.MESH
ROUNDER = 12582912.0
COS = (0.999999989, -19.7392045, 64.9391159, -85.4501134, 60.1674298, -25.9668846, 6.52770596)
SIN = (6.2831853, -41.3417004, 81.6051308, -76.7030056, 42.0258515, -14.8995784, 3.23778009)


def horner(coefficients, x):
    total = coefficients[-1]
    for c in coefficients[-2::-1]:
        total = total * x + c
    return total


def turn(t):
    r = t - ((t + ROUNDER) - ROUNDER)
    x = r * r
    return horner(COS, x), r * horner(SIN, x)


def rotate(block):
    half = block.shape[1] // 2
    rolled = pltpu.roll(block, half, 1)
    lane = lax.broadcasted_iota(jnp.int32, block.shape, 1)
    return jnp.where(lane < half, -rolled, rolled)


def kernel(
    devices, norm,
    pp_ref, ph_ref, pf_ref, fp_ref, fh_ref, dc_ref, w_ref, out_ref,
    pk, wbuf, gbuf, fbuf, pcol, dcol, fcol, acc, mine, give, take, cbuf, psend, precv,
    pk_send, pk_recv, w_send, w_recv, w_own, x_send, x_recv, c_send, c_recv, p_send, p_recv,
):
    lines, halves = devices // GROUP, devices // 2
    points, sources, dirs = pp_ref.shape[1], fp_ref.shape[1], dc_ref.shape[1]
    me = lax.axis_index("refl")
    line, g = lax.div(me, GROUP), lax.rem(me, GROUP)
    half, core = lax.div(me, 2), lax.rem(me, 2)
    partner = half * 2 + (1 - core)

    def copy(src, dst, send, recv, to):
        return pltpu.make_async_remote_copy(
            src_ref=src, dst_ref=dst, send_sem=send, recv_sem=recv,
            device_id={"refl": to}, device_id_type=MESH,
        )

    halfs = [lax.rem(half + k, halves) for k in range(1, halves)]
    row = lax.rem(half, 2)
    across = (line * 2 + (1 - row)) * 2 + (1 - core)
    peers = [h * 2 + core for h in halfs] + [partner, across]

    barrier = pltpu.get_barrier_semaphore()
    for peer in peers:
        pl.semaphore_signal(barrier, inc=1, device_id={"refl": peer}, device_id_type=MESH)
    own_w = pltpu.make_async_copy(w_ref, wbuf.at[half], w_own)
    own_w.start()

    u, v = dc_ref[0:1, :], dc_ref[1:2, :]
    pk[me, :, :] = jnp.zeros((8, pk.shape[2]), jnp.float32)
    pk[me, 0:2, 0:points] = pp_ref[...]
    pk[me, 2:3, 0:points] = ph_ref[...]
    pk[me, 3:4, 0:points] = pf_ref[...] * norm
    pk[me, 4:6, 0:sources] = fp_ref[...]
    pk[me, 6:7, 0:sources] = fh_ref[...]
    pk[me, 4:6, sources:sources + dirs] = dc_ref[...]
    pk[me, 6:7, sources:sources + dirs] = jnp.sqrt(1.0 - u * u - v * v)

    pl.semaphore_wait(barrier, len(peers))

    pk_out = [
        copy(pk.at[me], pk.at[me], pk_send.at[i], pk_recv.at[me], peer)
        for i, peer in enumerate(peers)
    ]
    for c in pk_out:
        c.start()
    w_out = [
        copy(w_ref, wbuf.at[half], w_send.at[i], w_recv.at[half], h * 2 + core)
        for i, h in enumerate(halfs)
    ]
    for c in w_out:
        c.start()
    for i, peer in enumerate(peers):
        copy(pk.at[me], pk.at[peer], pk_send.at[i], pk_recv.at[peer], peer).wait_recv()

    for t in range(2):
        columns = jnp.transpose(pk[half * 2 + t])
        for j in range(3):
            pcol[j, t * points:(t + 1) * points, :] = jnp.broadcast_to(
                columns[0:points, j:j + 1], (points, LANES))
    columns = jnp.transpose(pk[me])
    fcol[...] = jnp.broadcast_to(columns[0:points, 3:4], (points, LANES))
    for t in range(GROUP):
        columns = jnp.transpose(pk[line * GROUP + t])
        for j in range(3):
            dcol[j, t * dirs:(t + 1) * dirs, :] = jnp.broadcast_to(
                columns[sources:sources + dirs, 4 + j:5 + j], (dirs, LANES))

    far_rows = GROUP * dirs

    def far(i, carry):
        at = lax.div(i, far_rows // ROWS)
        r = pl.multiple_of(lax.rem(i, far_rows // ROWS) * ROWS, ROWS)
        block = pk.at[at * GROUP + g]
        uc, vc, wc = dcol[0, pl.ds(r, ROWS), :], dcol[1, pl.ds(r, ROWS), :], dcol[2, pl.ds(r, ROWS), :]
        for j in range(points // LANES):
            lane = slice(j * LANES, (j + 1) * LANES)
            t = uc * block[0:1, lane] + vc * block[1:2, lane] + wc * block[2:3, lane]
            c, s = turn(t)
            fbuf[at, pl.ds(r, ROWS), lane] = c.astype(jnp.bfloat16)
            fbuf[at, pl.ds(far_rows + r, ROWS), lane] = s.astype(jnp.bfloat16)
        return carry

    near_rows = 2 * points

    def near(i, carry):
        at = lax.div(i, near_rows // ROWS)
        r = pl.multiple_of(lax.rem(i, near_rows // ROWS) * ROWS, ROWS)
        px, py, pz = pcol[0, pl.ds(r, ROWS), :], pcol[1, pl.ds(r, ROWS), :], pcol[2, pl.ds(r, ROWS), :]
        for y in range(2):
            block = pk.at[at * GROUP + y * 2 + core]
            for j in range(sources // LANES):
                lane = slice(j * LANES, (j + 1) * LANES)
                a = px - block[4:5, lane]
                b = py - block[5:6, lane]
                h = block[6:7, lane] - pz
                q = a * a + b * b + h * h
                inverse = lax.rsqrt(q)
                amplitude = (RANGE_REF * h) * (inverse * inverse)
                c, s = turn(q * inverse)
                to = slice(y * sources + j * LANES, y * sources + (j + 1) * LANES)
                gbuf[at, pl.ds(r, ROWS), to] = (amplitude * c).astype(jnp.bfloat16)
                gbuf[at, pl.ds(near_rows + r, ROWS), to] = (-amplitude * s).astype(jnp.bfloat16)
        return carry

    lax.fori_loop(0, lines * (near_rows // ROWS), near, 0)
    lax.fori_loop(0, lines * (far_rows // ROWS), far, 0)

    def weights_from(h):
        copy(w_ref, wbuf.at[h], w_send.at[0], w_recv.at[h], h * 2 + core).wait_recv()

    def near_dot(at):
        w = wbuf[pl.ds(at * 2, 2)].reshape(2 * sources, wbuf.shape[2])
        return jnp.dot(gbuf[at], w, preferred_element_type=jnp.float32)

    own_w.wait()
    weights_from(line * 2 + (1 - row))
    acc[...] = near_dot(line)

    def near_step(k, carry):
        at = lax.rem(line + k, lines)
        weights_from(at * 2)
        weights_from(at * 2 + 1)
        acc[...] += near_dot(at)
        return carry

    lax.fori_loop(1, lines, near_step, 0)

    def incident(t):
        r = pl.multiple_of(t * points, points)
        return acc[pl.ds(r, points), :] + rotate(acc[pl.ds(near_rows + r, points), :])

    give[...] = incident(1 - core)
    swap = copy(give, take, x_send, x_recv, partner)
    swap.start()
    mine[...] = incident(core)
    swap.wait_recv()
    cbuf[line] = ((mine[...] + take[...]) * fcol[...]).astype(jnp.bfloat16)

    c_out = [
        copy(cbuf.at[line], cbuf.at[line], c_send.at[k - 1], c_recv.at[line],
             lax.rem(line + k, lines) * GROUP + g)
        for k in range(1, lines)
    ]
    for c in c_out:
        c.start()

    acc2 = acc
    acc2[...] = jnp.dot(fbuf[line], cbuf[line], preferred_element_type=jnp.float32)

    def far_step(k, carry):
        at = lax.rem(line + k, lines)
        copy(cbuf.at[line], cbuf.at[at], c_send.at[0], c_recv.at[at], at * GROUP + g).wait_recv()
        acc2[...] += jnp.dot(fbuf[at], cbuf[at], preferred_element_type=jnp.float32)
        return carry

    lax.fori_loop(1, lines, far_step, 0)

    def pattern(t):
        r = pl.multiple_of(t * dirs, dirs)
        return acc2[pl.ds(r, dirs), :] + rotate(acc2[pl.ds(far_rows + r, dirs), :])

    others = [lax.rem(g + k, GROUP) for k in range(1, GROUP)]
    p_out = []
    for i, t in enumerate(others):
        psend[i] = pattern(t)
        c = copy(psend.at[i], precv.at[g], p_send.at[i], p_recv.at[g], line * GROUP + t)
        c.start()
        p_out.append(c)
    total = pattern(g)
    for i, t in enumerate(others):
        copy(psend.at[i], precv.at[t], p_send.at[i], p_recv.at[t], line * GROUP + t).wait_recv()
        total = total + precv[t]
    out_ref[...] = total

    for c in pk_out + w_out + [swap] + c_out + p_out:
        c.wait_send()


def per_device(
    feed_plane, feed_height, feed_weights, point_plane, point_height, patch_factor,
    direction_cosines,
):
    devices = lax.axis_size("refl")
    lines, halves = devices // GROUP, devices // 2
    points, sources, dirs = point_plane.shape[1], feed_plane.shape[1], direction_cosines.shape[1]
    columns = feed_weights.shape[1]
    width = max(points, sources + dirs)
    near_rows, far_rows = 2 * points, GROUP * dirs
    f32, bf16 = jnp.float32, jnp.bfloat16
    dma = pltpu.SemaphoreType.DMA
    vmem = pl.BlockSpec(memory_space=pltpu.VMEM)
    norm = 1.0 / math.sqrt(points * devices)
    return pl.pallas_call(
        functools.partial(kernel, devices, norm),
        out_shape=jax.ShapeDtypeStruct((dirs, columns), f32),
        in_specs=[vmem] * 6 + [pl.BlockSpec(memory_space=pl.ANY)],
        out_specs=vmem,
        scratch_shapes=[
            pltpu.VMEM((devices, 8, width), f32),
            pltpu.VMEM((halves, sources, columns), bf16),
            pltpu.VMEM((lines, 2 * near_rows, 2 * sources), bf16),
            pltpu.VMEM((lines, 2 * far_rows, points), bf16),
            pltpu.VMEM((3, near_rows, LANES), f32),
            pltpu.VMEM((3, far_rows, LANES), f32),
            pltpu.VMEM((points, LANES), f32),
            pltpu.VMEM((2 * max(near_rows, far_rows), columns), f32),
            pltpu.VMEM((points, columns), f32),
            pltpu.VMEM((points, columns), f32),
            pltpu.VMEM((points, columns), f32),
            pltpu.VMEM((lines, points, columns), bf16),
            pltpu.VMEM((GROUP - 1, dirs, columns), f32),
            pltpu.VMEM((GROUP, dirs, columns), f32),
            dma((halves + 1,)), dma((devices,)),
            dma((halves - 1,)), dma((halves,)), dma,
            dma, dma,
            dma((lines - 1,)), dma((lines,)),
            dma((GROUP - 1,)), dma((GROUP,)),
        ],
        compiler_params=pltpu.CompilerParams(collective_id=0, has_side_effects=True),
    )(
        point_plane, point_height.reshape(1, -1), patch_factor.reshape(1, -1),
        feed_plane, feed_height.reshape(1, -1), direction_cosines, feed_weights,
    )


def solution(mesh):
    in_specs = (
        P("grp", "refl"),
        P(("grp", "refl")),
        P("refl", "grp"),
        P("grp", "refl"),
        P(("grp", "refl")),
        P(("grp", "refl")),
        P(None, "refl"),
    )
    return jax.shard_map(
        per_device, mesh=mesh, in_specs=in_specs, out_specs=P("refl", "grp"), check_vma=False
    )
```

```python
import functools
import math

import jax
import jax.numpy as jnp
from jax import lax
from jax.experimental import pallas as pl
from jax.experimental.pallas import tpu as pltpu
from jax.sharding import PartitionSpec as P

RANGE_REF = 20.0
GROUP = 4
LANES = 128
ROWS = 32
MESH = pl.DeviceIdType.MESH
ROUNDER = 12582912.0
COS = (1.4142135, -6.97885091, 5.73945958, -1.88355282, 0.310677863)
SIN = (4.44288292, -7.30824568, 3.60635403, -0.846110414, 0.109822044)


def horner(coefficients, x):
    total = coefficients[-1]
    for c in coefficients[-2::-1]:
        total = total * x + c
    return total


def turn(t):
    r = t - ((t + ROUNDER) - ROUNDER)
    x = r * r
    s = r * horner(SIN, x)
    return 1.0 - s * s, s * horner(COS, x)


def rotate(block):
    half = block.shape[1] // 2
    rolled = pltpu.roll(block, half, 1)
    lane = lax.broadcasted_iota(jnp.int32, block.shape, 1)
    return jnp.where(lane < half, -rolled, rolled)


def kernel(
    devices, norm,
    pp_in, ph_in, pf_in, fp_in, fh_in, dc_in, w_in, out_ref,
    pp_ref, ph_ref, pf_ref, fp_ref, fh_ref, dc_ref,
    pk, wbuf, gbuf, fbuf, pcol, dcol, fcol, acc, give, take, cbuf, psend, precv,
    in_sem, pk_send, pk_recv, w_send, w_recv, w_own, x_send, x_recv, p_send, p_recv,
):
    lines, halves = devices // GROUP, devices // 2
    points, sources, dirs = pp_in.shape[1], fp_in.shape[1], dc_in.shape[1]
    me = lax.axis_index("refl")
    line, g = lax.div(me, GROUP), lax.rem(me, GROUP)
    half, core = lax.div(me, 2), lax.rem(me, 2)
    row = lax.rem(half, 2)
    partner = half * 2 + (1 - core)
    beside = (line * 2 + (1 - row)) * 2 + core
    across = (line * 2 + (1 - row)) * 2 + (1 - core)

    def copy(src, dst, send, recv, to):
        return pltpu.make_async_remote_copy(
            src_ref=src, dst_ref=dst, send_sem=send, recv_sem=recv,
            device_id={"refl": to}, device_id_type=MESH,
        )

    offsets = sorted(range(1, lines), key=lambda k: (-min(k, lines - k), k))
    same_core = []
    for k in offsets:
        at = lax.rem(line + k, lines)
        same_core += [at * GROUP + (1 - row) * 2 + core, at * GROUP + g]
    same_core += [beside]
    peers = same_core + [across, partner]

    barrier = pltpu.get_barrier_semaphore()
    for peer in peers:
        pl.semaphore_signal(barrier, inc=1, device_id={"refl": peer}, device_id_type=MESH)
    own_w = pltpu.make_async_copy(w_in, wbuf.at[half], w_own)
    own_w.start()
    loads = [
        pltpu.make_async_copy(a, b, in_sem.at[i])
        for i, (a, b) in enumerate((
            (pp_in, pp_ref), (ph_in, ph_ref), (pf_in, pf_ref),
            (fp_in, fp_ref), (fh_in, fh_ref), (dc_in, dc_ref),
        ))
    ]
    for c in loads:
        c.start()
    for c in loads:
        c.wait()

    u, v = dc_ref[0:1, :], dc_ref[1:2, :]
    pk[me, :, :] = jnp.zeros((8, pk.shape[2]), jnp.float32)
    pk[me, 0:2, 0:points] = pp_ref[...]
    pk[me, 2:3, 0:points] = ph_ref[...]
    pk[me, 3:4, 0:points] = pf_ref[...] * norm
    pk[me, 4:6, 0:sources] = fp_ref[...]
    pk[me, 6:7, 0:sources] = fh_ref[...]
    pk[me, 4:6, sources:sources + dirs] = dc_ref[...]
    pk[me, 6:7, sources:sources + dirs] = jnp.sqrt(1.0 - u * u - v * v)

    pl.semaphore_wait(barrier, len(peers))

    pk_out = [
        copy(pk.at[me], pk.at[me], pk_send.at[i], pk_recv.at[me], peer)
        for i, peer in enumerate(peers)
    ]
    for c in pk_out:
        c.start()
    w_out = [
        copy(w_in, wbuf.at[half], w_send.at[i], w_recv.at[half], peer)
        for i, peer in enumerate(same_core)
    ]
    for c in w_out:
        c.start()

    def pack_from(peer):
        copy(pk.at[me], pk.at[peer], pk_send.at[0], pk_recv.at[peer], peer).wait_recv()

    for peer in (partner, beside, across):
        pack_from(peer)

    near_rows = GROUP * points
    for t in range(GROUP):
        columns = jnp.transpose(pk[line * GROUP + t])
        rows = slice(t * points, (t + 1) * points)
        for j in range(3):
            pcol[j, rows, :] = jnp.broadcast_to(columns[0:points, j:j + 1], (points, LANES))
        fcol[rows, :] = jnp.broadcast_to(columns[0:points, 3:4], (points, LANES))

    def near_block(at):
        def near(i, carry):
            r = pl.multiple_of(i * ROWS, ROWS)
            px, py, pz = pcol[0, pl.ds(r, ROWS), :], pcol[1, pl.ds(r, ROWS), :], pcol[2, pl.ds(r, ROWS), :]
            for y in range(2):
                block = pk.at[at * GROUP + y * 2 + core]
                for j in range(sources // LANES):
                    lane = slice(j * LANES, (j + 1) * LANES)
                    a = px - block[4:5, lane]
                    b = py - block[5:6, lane]
                    h = block[6:7, lane] - pz
                    q = a * a + b * b + h * h
                    inverse = lax.rsqrt(q)
                    amplitude = (RANGE_REF * h) * (inverse * inverse)
                    c, s = turn(q * inverse)
                    to = slice(y * sources + j * LANES, y * sources + (j + 1) * LANES)
                    gbuf[at, pl.ds(r, ROWS), to] = (amplitude * c).astype(jnp.bfloat16)
                    gbuf[at, pl.ds(near_rows + r, ROWS), to] = (-amplitude * s).astype(jnp.bfloat16)
            return carry

        lax.fori_loop(0, near_rows // ROWS, near, 0)

    def near_line(k, carry):
        at = lax.rem(line + k, lines)

        @pl.when(k > 0)
        def _():
            pack_from(at * GROUP + core)
            pack_from(at * GROUP + 2 + core)

        near_block(at)
        return carry

    lax.fori_loop(0, lines, near_line, 0)

    def weights_from(h):
        copy(w_in, wbuf.at[h], w_send.at[0], w_recv.at[h], h * 2 + core).wait_recv()

    def near_dot(at):
        w = wbuf[pl.ds(at * 2, 2)].reshape(2 * sources, wbuf.shape[2])
        return jnp.dot(gbuf[at], w, preferred_element_type=jnp.float32)

    own_w.wait()
    weights_from(line * 2 + (1 - row))
    acc[...] = near_dot(line)

    def near_step(k, carry):
        at = lax.rem(line + k, lines)
        weights_from(at * 2)
        weights_from(at * 2 + 1)
        acc[...] += near_dot(at)
        return carry

    lax.fori_loop(1, lines, near_step, 0)

    swaps = []
    for t in range(GROUP):
        rows = slice(t * points, (t + 1) * points)
        give[t] = acc[rows, :] + rotate(acc[near_rows + t * points:near_rows + (t + 1) * points, :])
        c = copy(give.at[t], take.at[t], x_send.at[t], x_recv.at[t], partner)
        c.start()
        swaps.append(c)

    def far_block(at):
        columns = jnp.transpose(pk[at * GROUP + g])
        for j in range(3):
            dcol[j] = jnp.broadcast_to(
                columns[sources:sources + dirs, 4 + j:5 + j], (dirs, LANES))

        def far(i, carry):
            t = lax.div(i, dirs // ROWS)
            r = pl.multiple_of(lax.rem(i, dirs // ROWS) * ROWS, ROWS)
            block = pk.at[line * GROUP + t]
            uc, vc, wc = dcol[0, pl.ds(r, ROWS), :], dcol[1, pl.ds(r, ROWS), :], dcol[2, pl.ds(r, ROWS), :]
            for j in range(points // LANES):
                lane = slice(j * LANES, (j + 1) * LANES)
                c, s = turn(uc * block[0:1, lane] + vc * block[1:2, lane] + wc * block[2:3, lane])
                fbuf[at, t, pl.ds(r, ROWS), lane] = c.astype(jnp.bfloat16)
                fbuf[at, t, pl.ds(dirs + r, ROWS), lane] = s.astype(jnp.bfloat16)
            return carry

        lax.fori_loop(0, GROUP * (dirs // ROWS), far, 0)

    def far_dot(at):
        both = jnp.dot(fbuf[at, 0], cbuf[0], preferred_element_type=jnp.float32)
        for t in range(1, GROUP):
            both += jnp.dot(fbuf[at, t], cbuf[t], preferred_element_type=jnp.float32)
        return both[0:dirs, :] + rotate(both[dirs:2 * dirs, :])

    order = [lax.rem(line + k, lines) for k in offsets]
    ahead = min(2, len(order))
    for at in order[:ahead]:
        far_block(at)

    for t in range(GROUP):
        swaps[t].wait_recv()
        rows = slice(t * points, (t + 1) * points)
        cbuf[t] = ((give[t] + take[t]) * fcol[rows, :]).astype(jnp.bfloat16)

    p_out = []
    for i, at in enumerate(order):
        if i >= ahead:
            far_block(at)
        psend[i] = far_dot(at).astype(jnp.bfloat16)
        c = copy(psend.at[i], precv.at[line], p_send.at[i], p_recv.at[line], at * GROUP + g)
        c.start()
        p_out.append(c)
    far_block(line)
    total = far_dot(line)
    for i, at in reversed(list(enumerate(order))):
        copy(psend.at[i], precv.at[at], p_send.at[i], p_recv.at[at], at * GROUP + g).wait_recv()
        total = total + precv[at].astype(jnp.float32)
    out_ref[...] = total

    for c in pk_out + w_out + swaps + p_out:
        c.wait_send()


def per_device(
    feed_plane, feed_height, feed_weights, point_plane, point_height, patch_factor,
    direction_cosines,
):
    devices = lax.axis_size("refl")
    lines, halves = devices // GROUP, devices // 2
    points, sources, dirs = point_plane.shape[1], feed_plane.shape[1], direction_cosines.shape[1]
    columns = feed_weights.shape[1]
    width = max(points, sources + dirs)
    near_rows = GROUP * points
    f32, bf16 = jnp.float32, jnp.bfloat16
    dma = pltpu.SemaphoreType.DMA
    norm = 1.0 / math.sqrt(points * devices)
    return pl.pallas_call(
        functools.partial(kernel, devices, norm),
        out_shape=jax.ShapeDtypeStruct((dirs, columns), f32),
        in_specs=[pl.BlockSpec(memory_space=pl.ANY)] * 7,
        out_specs=pl.BlockSpec(memory_space=pltpu.VMEM),
        scratch_shapes=[
            pltpu.VMEM((2, points), f32), pltpu.VMEM((1, points), f32), pltpu.VMEM((1, points), f32),
            pltpu.VMEM((2, sources), f32), pltpu.VMEM((1, sources), f32), pltpu.VMEM((2, dirs), f32),
            pltpu.VMEM((devices, 8, width), f32),
            pltpu.VMEM((halves, sources, columns), bf16),
            pltpu.VMEM((lines, 2 * near_rows, 2 * sources), bf16),
            pltpu.VMEM((lines, GROUP, 2 * dirs, points), bf16),
            pltpu.VMEM((3, near_rows, LANES), f32),
            pltpu.VMEM((3, dirs, LANES), f32),
            pltpu.VMEM((near_rows, LANES), f32),
            pltpu.VMEM((2 * near_rows, columns), f32),
            pltpu.VMEM((GROUP, points, columns), f32),
            pltpu.VMEM((GROUP, points, columns), f32),
            pltpu.VMEM((GROUP, points, columns), bf16),
            pltpu.VMEM((lines - 1, dirs, columns), bf16),
            pltpu.VMEM((lines, dirs, columns), bf16),
            dma((6,)), dma((halves + 1,)), dma((devices,)),
            dma((halves - 1,)), dma((halves,)), dma,
            dma((GROUP,)), dma((GROUP,)),
            dma((lines - 1,)), dma((lines,)),
        ],
        compiler_params=pltpu.CompilerParams(collective_id=0, has_side_effects=True),
    )(
        point_plane, point_height.reshape(1, -1), patch_factor.reshape(1, -1),
        feed_plane, feed_height.reshape(1, -1), direction_cosines, feed_weights,
    )


def solution(mesh):
    in_specs = (
        P("grp", "refl"),
        P(("grp", "refl")),
        P("refl", "grp"),
        P("grp", "refl"),
        P(("grp", "refl")),
        P(("grp", "refl")),
        P(None, "refl"),
    )
    return jax.shard_map(
        per_device, mesh=mesh, in_specs=in_specs, out_specs=P("refl", "grp"), check_vma=False
    )
```
